128 devices in a mesh: row: 8 (over z, y_lo), col: 16 (over x, y_hi, core).
Axes of the slice: x: 4, y: 4 (y_hi: 2, y_lo: 2; y = y_hi * 2 + y_lo), z: 4, core: 2. Of those that a mesh axis runs over, the one named last changes fastest.
Arguments:
- t2_amps: bfloat16 [16384, 2048], P('row', 'col'), may hold values from -6 to 6
- v_ints: bfloat16 [2048, 32768], P('row', 'col'), may hold values from -0.125 to 0.125
- t2_mask: int32 [128, 16], P('row', 'col'), may hold values 0 or 1
- v_mask: int32 [16, 256], P('row', 'col'), may hold values 0 or 1
Outputs:
- ladder: bfloat16 [16384, 32768], P('row', 'col')
The draws below stay inside these ranges and needn't reach their ends.
All inputs are finite; a program needn't handle non-finite values. No bound on the sum of `t2_mask` or of `v_mask` on one device may be relied on, other than what follows from the above.
Results may differ from the reference program's by a relative error of at most 0.001.
Values may be sent and summed in bfloat16 or wider, within the bound.
A program may use at most 64 MiB of HBM per device.

```python
import jax
import jax.numpy as jnp
from jax import lax

TILE = 128
CD_TILES = 16
IJ_DEV = 2048
CD = 2048
IJ = 16384
AB = 32768
N_ROW = 8


def plant(entries, rng, low, largest):
    longest = entries.shape.index(max(entries.shape))
    spots = []
    for shift in (0, 1):
        where = [jax.random.randint(jax.random.fold_in(rng, axis), (), 0, length) for axis, length in enumerate(entries.shape)]
        where[longest] = (where[longest] + shift) % entries.shape[longest]
        spots.append(tuple(where))
    return entries.at[spots[0]].set(low).at[spots[1]].set(largest)


def level_of(stream_key, dims, pieces, least, top_value):
    loudness = 1.0
    for dim, blocks in pieces:
        draws = jax.random.uniform(jax.random.fold_in(jax.random.fold_in(stream_key, 6), dim), (blocks,), jnp.float32, least / len(pieces), top_value / len(pieces))
        loudness = loudness * jnp.repeat(jnp.exp(draws), dims[dim] // blocks).reshape((-1,) + (1,) * (len(dims) - 1 - dim))
    return loudness


def noise(rng, extent, deviation, reach, cuts=(), held_as=jnp.bfloat16):
    result = deviation * jax.random.normal(rng, extent, jnp.float32)
    if cuts:
        result = result * level_of(rng, extent, cuts, -0.22, 0.18)
    return jnp.clip(result, -reach, reach).astype(held_as)


def setup_inputs(seed: int = 0) -> dict:
    key_of = jax.random.split(jax.random.key(seed), 5)
    t2_amps = noise(key_of[0], (IJ, CD), 1.0, 6.0, ((0, 8), (1, 16)))
    v_ints = noise(key_of[1], (CD, AB), CD ** -0.5, 0.125, ((0, 8), (1, 16)))
    t2_mask = plant((jax.random.randint(key_of[2], (IJ // TILE, CD_TILES), 0, 4) < 3).astype(jnp.int32), jax.random.fold_in(key_of[2], 1), 0, 1)
    v_mask = plant((jax.random.randint(key_of[3], (CD_TILES, AB // TILE), 0, 4) < 3).astype(jnp.int32), jax.random.fold_in(key_of[3], 1), 0, 1)
    return dict(t2_amps=t2_amps, v_ints=v_ints, t2_mask=t2_mask, v_mask=v_mask)


def expand(mask, rows, cols):
    kept = jnp.broadcast_to(mask[:, None, :, None] > 0, (mask.shape[0], TILE, mask.shape[1], TILE))
    return kept.reshape(rows, cols)


def reference(t2_amps, v_ints, t2_mask, v_mask):
    masked_t2 = jnp.where(expand(t2_mask, IJ, CD), t2_amps, jnp.zeros_like(t2_amps))
    masked_v = jnp.where(expand(v_mask, CD, AB), v_ints, jnp.zeros_like(v_ints))
    blocks = masked_t2.reshape(N_ROW, IJ_DEV, CD)

    def one_block(block):
        return jnp.dot(block, masked_v, preferred_element_type=jnp.float32).astype(jnp.bfloat16)

    ladder = lax.map(one_block, blocks)
    return ladder.reshape(IJ, AB)
```

```python
import jax
import jax.numpy as jnp
from jax import lax
from jax.experimental import pallas as pl
from jax.experimental.pallas import tpu as pltpu
from jax.sharding import PartitionSpec as P

TILE = 128
CHUNK = 256
N_CHUNK = 8
EARLY = 7
PIECE = 256
QROWS = 512
N_Q = 4
CD = 2048
IJ = 2048
MESH = pl.DeviceIdType.MESH


def mask_kernel(t2_mask, v_mask, t2, v, t2_out, v_out):
    for i in range(IJ // TILE):
        rows = pl.ds(i * TILE, TILE)
        block = t2[rows, :]
        t2_out[rows, :] = jnp.where(t2_mask[i, 0] > 0, block, jnp.zeros_like(block))
    for j in range(N_CHUNK):
        for b in range(CHUNK // TILE):
            for i in range(PIECE // TILE):
                rows = pl.ds(i * TILE, TILE)
                block = v[rows, pl.ds(j * CHUNK + b * TILE, TILE)]
                kept = v_mask[i, j * (CHUNK // TILE) + b] > 0
                v_out[j, rows, pl.ds(b * TILE, TILE)] = jnp.where(kept, block, jnp.zeros_like(block))


def product(t_all, v_all, j, rows):
    amps = jnp.concatenate([t_all[p, rows, :] for p in range(CD // TILE)], axis=1)
    return jnp.dot(amps, v_all[j], preferred_element_type=jnp.float32).astype(jnp.bfloat16)


COPIES = {
    "zp_own": N_CHUNK, "zm_own": N_CHUNK, "zp_far": N_CHUNK, "zm_far": N_CHUNK,
    "zp_pair": N_CHUNK, "zm_pair": N_CHUNK, "y_own": N_CHUNK, "y_far": N_CHUNK,
    "t_y": N_Q, "xp_own": N_Q, "xm_own": N_Q, "xp_y": N_Q, "xm_y": N_Q,
    "xp_far": N_Q // 2, "xm_far": N_Q // 2, "xp_yfar": N_Q // 2, "xm_yfar": N_Q // 2,
    "core": 8 * N_Q,
}
FIRST = {}
for _name, _count in COPIES.items():
    FIRST[_name] = sum(COPIES[n] for n in list(COPIES)[: list(COPIES).index(_name)])
N_COPIES = sum(COPIES.values())


def gather_kernel(t_own, v_own, t_all, v_all, early, send, recv, local):
    row, col = lax.axis_index("row"), lax.axis_index("col")
    z, y_lo = row // 2, row % 2
    x, y_hi, core = col // 4, (col // 2) % 2, col % 2

    def at_row(dz, flip=False):
        return ((z + dz) % 4) * 2 + (1 - y_lo if flip else y_lo)

    def at_col(dx, flip=False, other=False):
        return ((x + dx) % 4) * 4 + (1 - y_hi if flip else y_hi) * 2 + (1 - core if other else core)

    to = {
        "zp": (at_row(1), col), "zm": (at_row(3), col), "y": (at_row(0, True), col),
        "xp": (row, at_col(1)), "xm": (row, at_col(3)), "t": (row, at_col(0, True)),
        "core": (row, at_col(0, False, True)),
    }

    def v_slot(j, piece, first=0, count=PIECE):
        return v_all.at[j, pl.ds(pl.multiple_of(piece * PIECE + first, 128), count), :]

    def t_slot(piece, q):
        return t_all.at[piece, pl.ds(q * QROWS, QROWS), :]

    started = []

    def describe(name, n, src, dst):
        i = FIRST[name] + n
        return pltpu.make_async_remote_copy(
            src_ref=src, dst_ref=dst, send_sem=send.at[i], recv_sem=recv.at[i],
            device_id=to[name.split("_")[0]], device_id_type=MESH,
        )

    def put(name, n, src, dst):
        copy = describe(name, n, src, dst)
        copy.start()
        started.append(copy)

    def got(name, n, slot):
        describe(name, n, slot, slot).wait_recv()

    def share(n, q, piece, src=None):
        put("core", n * N_Q + q, t_slot(piece, q) if src is None else src, t_slot(piece, q))

    keep_t = pltpu.make_async_copy(t_own, t_all.at[col], local.at[0])
    keep_v = [pltpu.make_async_copy(v_own.at[j], v_slot(j, row), local.at[1 + j]) for j in range(N_CHUNK)]

    barrier = pltpu.get_barrier_semaphore()
    for device in to.values():
        pl.semaphore_signal(barrier, inc=1, device_id=device, device_id_type=MESH)
    keep_t.start()
    for copy in keep_v:
        copy.start()
    pl.semaphore_wait(barrier, len(to))

    for q in range(N_Q):
        put("t_y", q, t_own.at[pl.ds(q * QROWS, QROWS), :], t_slot(col, q))
    for j in range(N_CHUNK):
        put("zp_own", j, v_own.at[j], v_slot(j, row))
        put("zm_own", j, v_own.at[j], v_slot(j, row))
    for q in range(N_Q):
        put("xp_own", q, t_own.at[pl.ds(q * QROWS, QROWS), :], t_slot(col, q))
        put("xm_own", q, t_own.at[pl.ds(q * QROWS, QROWS), :], t_slot(col, q))
    for j in range(N_CHUNK):
        put("y_own", j, v_own.at[j], v_slot(j, row))
    for q in range(N_Q):
        share(0, q, col, t_own.at[pl.ds(q * QROWS, QROWS), :])

    below, above = at_row(3), at_row(1)
    left, right = at_col(3), at_col(1)
    across = at_col(0, True)
    for j in range(N_CHUNK):
        got("zp_own", j, v_slot(j, below))
        got("zm_own", j, v_slot(j, above))
        put("zp_far", j, v_slot(j, below, 0, 128), v_slot(j, below, 0, 128))
        put("zm_far", j, v_slot(j, above, 128, 128), v_slot(j, above, 128, 128))
        if j < N_Q:
            q = j
            got("xp_own", q, t_slot(left, q))
            got("xm_own", q, t_slot(right, q))
            if q < N_Q // 2:
                put("xp_far", q, t_slot(left, q), t_slot(left, q))
            else:
                put("xm_far", q - N_Q // 2, t_slot(right, q), t_slot(right, q))
            share(1, q, left)
            share(2, q, right)
        else:
            q = j - N_Q
            got("t_y", q, t_slot(across, q))
            put("xp_y", q, t_slot(across, q), t_slot(across, q))
            put("xm_y", q, t_slot(across, q), t_slot(across, q))
            share(3, q, across)

    far = at_col(2)
    for q in range(N_Q):
        if q < N_Q // 2:
            got("xp_far", q, t_slot(far, q))
        else:
            got("xm_far", q - N_Q // 2, t_slot(far, q))
        share(4, q, far)

    pair = at_row(0, True)
    opposite = at_row(2)

    def far_on(j):
        got("zp_far", j, v_slot(j, opposite, 0, 128))
        got("zm_far", j, v_slot(j, opposite, 128, 128))
        put("y_far", j, v_slot(j, opposite), v_slot(j, opposite))

    y_left, y_right, y_far = at_col(3, True), at_col(1, True), at_col(2, True)
    for j in range(N_CHUNK):
        got("y_own", j, v_slot(j, pair))
        put("zp_pair", j, v_slot(j, pair), v_slot(j, pair))
        put("zm_pair", j, v_slot(j, pair), v_slot(j, pair))
        if j < N_Q:
            q = j
            got("xp_y", q, t_slot(y_left, q))
            got("xm_y", q, t_slot(y_right, q))
            if q < N_Q // 2:
                put("xp_yfar", q, t_slot(y_left, q), t_slot(y_left, q))
            else:
                put("xm_yfar", q - N_Q // 2, t_slot(y_right, q), t_slot(y_right, q))
            share(5, q, y_left)
            share(6, q, y_right)
        else:
            far_on(2 * (j - N_Q))
            far_on(2 * (j - N_Q) + 1)
    for q in range(N_Q):
        if q < N_Q // 2:
            got("xp_yfar", q, t_slot(y_far, q))
        else:
            got("xm_yfar", q - N_Q // 2, t_slot(y_far, q))
        share(7, q, y_far)

    other = [at_col(dx, flip, True) for dx, flip in
             ((0, False), (3, False), (1, False), (0, True), (2, False), (3, True), (1, True), (2, True))]
    for n in range(8):
        for q in range(N_Q):
            got("core", n * N_Q + q, t_slot(other[n], q))
    keep_t.wait()
    for copy in keep_v:
        copy.wait()

    def chunk_here(j):
        got("zp_pair", j, v_slot(j, at_row(3, True)))
        got("zm_pair", j, v_slot(j, at_row(1, True)))
        got("y_far", j, v_slot(j, at_row(2, True)))

    for j in range(N_CHUNK):
        chunk_here(j)
        if j < EARLY:
            early[j] = product(t_all, v_all, j, slice(None))
    for copy in started:
        copy.wait_send()


def last_kernel(t_all, v_all, early, out, tail, sems):
    copies = [
        pltpu.make_async_copy(early.at[j], out.at[:, pl.ds(j * CHUNK, CHUNK)], sems.at[j]) for j in range(EARLY)
    ]
    for copy in copies:
        copy.start()
    for j in range(EARLY, N_CHUNK):
        for m in range(2):
            rows = pl.ds(m * (IJ // 2), IJ // 2)
            tail[j - EARLY, rows, :] = product(t_all, v_all, j, rows)
            copy = pltpu.make_async_copy(
                tail.at[j - EARLY, rows, :], out.at[rows, pl.ds(j * CHUNK, CHUNK)],
                sems.at[EARLY + 2 * (j - EARLY) + m],
            )
            copy.start()
            copies.append(copy)
    for copy in copies:
        copy.wait()


def body(t2_amps, v_ints, t2_mask, v_mask):
    bf16 = jnp.bfloat16
    vmem = pl.BlockSpec(memory_space=pltpu.VMEM)
    smem = pl.BlockSpec(memory_space=pltpu.SMEM)
    t_own, v_own = pl.pallas_call(
        mask_kernel,
        out_shape=(pltpu.VMEM((IJ, TILE), bf16), pltpu.VMEM((N_CHUNK, PIECE, CHUNK), bf16)),
        in_specs=[smem, smem, vmem, vmem],
        out_specs=(vmem, vmem),
        compiler_params=pltpu.CompilerParams(vmem_limit_bytes=8 * 2**20),
        name="mask",
    )(t2_mask, v_mask, t2_amps, v_ints)
    inside = lambda a: pltpu.with_memory_space_constraint(a, pltpu.VMEM)
    t_all, v_all, early = pl.pallas_call(
        gather_kernel,
        out_shape=(
            pltpu.VMEM((CD // TILE, IJ, TILE), bf16),
            pltpu.VMEM((N_CHUNK, CD, CHUNK), bf16),
            pltpu.VMEM((EARLY, IJ, CHUNK), bf16),
        ),
        in_specs=[vmem, vmem],
        out_specs=(vmem, vmem, vmem),
        scratch_shapes=[
            pltpu.SemaphoreType.DMA((N_COPIES,)),
            pltpu.SemaphoreType.DMA((N_COPIES,)),
            pltpu.SemaphoreType.DMA((1 + N_CHUNK,)),
        ],
        compiler_params=pltpu.CompilerParams(
            collective_id=0, has_side_effects=True, vmem_limit_bytes=16 * 2**20
        ),
        name="gather",
    )(inside(t_own), inside(v_own))
    return pl.pallas_call(
        last_kernel,
        out_shape=jax.ShapeDtypeStruct((IJ, N_CHUNK * CHUNK), bf16),
        in_specs=[vmem, vmem, vmem],
        out_specs=pl.BlockSpec(memory_space=pl.ANY),
        scratch_shapes=[
            pltpu.VMEM((N_CHUNK - EARLY, IJ, CHUNK), bf16),
            pltpu.SemaphoreType.DMA((EARLY + 2 * (N_CHUNK - EARLY),)),
        ],
        compiler_params=pltpu.CompilerParams(vmem_limit_bytes=16 * 2**20),
        name="last",
    )(inside(t_all), inside(v_all), inside(early))


def solution(mesh):
    in_specs = (P("row", "col"), P("row", "col"), P("row", "col"), P("row", "col"))
    out_specs = P("row", "col")
    return jax.shard_map(body, mesh=mesh, in_specs=in_specs, out_specs=out_specs, check_vma=False)
```

```python
import jax
import jax.numpy as jnp
from jax import lax
from jax.experimental import pallas as pl
from jax.experimental.pallas import tpu as pltpu
from jax.sharding import PartitionSpec as P

TILE = 128
CHUNK = 256
N_CHUNK = 8
EARLY = 7
Y_FIRST = 3
PIECE = 256
QROWS = 512
N_Q = 4
CD = 2048
IJ = 2048
MESH = pl.DeviceIdType.MESH


def mask_kernel(t2_mask, v_mask, t2_hbm, v_hbm, t2_out, v_out, t2, v, sems):
    v_in = [
        pltpu.make_async_copy(v_hbm.at[pl.ds(i * TILE, TILE), :], v.at[pl.ds(i * TILE, TILE), :], sems.at[i])
        for i in range(PIECE // TILE)
    ]
    t_in = [
        pltpu.make_async_copy(
            t2_hbm.at[pl.ds(q * QROWS, QROWS), :], t2.at[pl.ds(q * QROWS, QROWS), :], sems.at[PIECE // TILE + q]
        )
        for q in range(N_Q)
    ]
    for copy in t_in + v_in:
        copy.start()
    for i in range(IJ // TILE):
        if i % (QROWS // TILE) == 0:
            t_in[i // (QROWS // TILE)].wait()
        rows = pl.ds(i * TILE, TILE)
        block = t2[rows, :]
        t2_out[rows, :] = jnp.where(t2_mask[i] > 0, block, jnp.zeros_like(block))
    for i in range(PIECE // TILE):
        v_in[i].wait()
        rows = pl.ds(i * TILE, TILE)
        for j in range(N_CHUNK):
            for b in range(CHUNK // TILE):
                block = v[rows, pl.ds(j * CHUNK + b * TILE, TILE)]
                kept = v_mask[i, j * (CHUNK // TILE) + b] > 0
                v_out[j, rows, pl.ds(b * TILE, TILE)] = jnp.where(kept, block, jnp.zeros_like(block))


def product(t_all, v_all, j, rows):
    amps = jnp.concatenate([t_all[p, rows, :] for p in range(CD // TILE)], axis=1)
    return jnp.dot(amps, v_all[j], preferred_element_type=jnp.float32).astype(jnp.bfloat16)


COPIES = {
    "zp_own": N_CHUNK, "zm_own": N_CHUNK, "zp_far": N_CHUNK, "zm_far": N_CHUNK,
    "zp_pair": N_CHUNK, "zm_pair": N_CHUNK, "y_own": N_CHUNK, "y_far": N_CHUNK,
    "b_t": N_Q, "y_t": N_Q, "xp_own": N_Q, "xm_own": N_Q, "xp_y": N_Q, "xm_y": N_Q,
    "xp_far": N_Q // 2, "xm_far": N_Q // 2, "xp_yfar": N_Q // 2, "xm_yfar": N_Q // 2,
    "core": 8 * N_Q,
}
FIRST = {}
for _name, _count in COPIES.items():
    FIRST[_name] = sum(COPIES[n] for n in list(COPIES)[: list(COPIES).index(_name)])
N_COPIES = sum(COPIES.values())


def gather_kernel(t_own, v_own, t_all, v_all, early, relay, send, recv, local):
    row, col = lax.axis_index("row"), lax.axis_index("col")
    z, y_lo = row // 2, row % 2
    x, y_hi, core = col // 4, (col // 2) % 2, col % 2

    def at_row(dz, flip=False):
        return ((z + dz) % 4) * 2 + (1 - y_lo if flip else y_lo)

    def at_col(dx, flip=False, other=False):
        return ((x + dx) % 4) * 4 + (1 - y_hi if flip else y_hi) * 2 + (1 - core if other else core)

    to = {
        "zp": (at_row(1), col), "zm": (at_row(3), col), "y": (at_row(0, True), col),
        "xp": (row, at_col(1)), "xm": (row, at_col(3)), "b": (at_row(0, True), at_col(0, True)),
        "core": (row, at_col(0, False, True)),
    }

    def v_slot(j, piece, first=0, count=PIECE):
        return v_all.at[j, pl.ds(pl.multiple_of(piece * PIECE + first, 128), count), :]

    def t_slot(piece, q):
        return t_all.at[piece, pl.ds(q * QROWS, QROWS), :]

    started = []

    def describe(name, n, src, dst):
        i = FIRST[name] + n
        return pltpu.make_async_remote_copy(
            src_ref=src, dst_ref=dst, send_sem=send.at[i], recv_sem=recv.at[i],
            device_id=to[name.split("_")[0]], device_id_type=MESH,
        )

    def put(name, n, src, dst):
        copy = describe(name, n, src, dst)
        copy.start()
        started.append(copy)

    def got(name, n, slot):
        describe(name, n, slot, slot).wait_recv()

    def share(n, q, piece, src=None):
        put("core", n * N_Q + q, t_slot(piece, q) if src is None else src, t_slot(piece, q))

    keep_t = pltpu.make_async_copy(t_own, t_all.at[col], local.at[0])
    keep_v = [pltpu.make_async_copy(v_own.at[j], v_slot(j, row), local.at[1 + j]) for j in range(N_CHUNK)]

    barrier = pltpu.get_barrier_semaphore()
    for device in to.values():
        pl.semaphore_signal(barrier, inc=1, device_id=device, device_id_type=MESH)
    keep_t.start()
    for copy in keep_v:
        copy.start()
    pl.semaphore_wait(barrier, len(to))

    def own_q(q):
        return t_own.at[pl.ds(q * QROWS, QROWS), :]

    def relay_q(q):
        return relay.at[pl.ds(q * QROWS, QROWS), :]

    def y_own(j):
        put("y_own", j, v_own.at[j], v_slot(j, row))

    for j in range(Y_FIRST):
        y_own(j)
    for q in range(N_Q):
        put("b_t", q, own_q(q), relay_q(q))
    for j in range(N_CHUNK):
        put("zp_own", j, v_own.at[j], v_slot(j, row))
        put("zm_own", j, v_own.at[j], v_slot(j, row))
    for q in range(N_Q):
        put("xp_own", q, own_q(q), t_slot(col, q))
        put("xm_own", q, own_q(q), t_slot(col, q))
    for q in range(N_Q):
        share(0, q, col, own_q(q))

    below, above = at_row(3), at_row(1)
    left, right = at_col(3), at_col(1)
    across = at_col(0, True)

    def v_far(j):
        got("zp_own", j, v_slot(j, below))
        got("zm_own", j, v_slot(j, above))
        put("zp_far", j, v_slot(j, below, 0, 128), v_slot(j, below, 0, 128))
        put("zm_far", j, v_slot(j, above, 128, 128), v_slot(j, above, 128, 128))

    for q in range(N_Q):
        got("b_t", q, relay_q(q))
        put("y_t", q, relay_q(q), t_slot(across, q))
        got("xp_own", q, t_slot(left, q))
        got("xm_own", q, t_slot(right, q))
        if q < N_Q // 2:
            put("xp_far", q, t_slot(left, q), t_slot(left, q))
        else:
            put("xm_far", q - N_Q // 2, t_slot(right, q), t_slot(right, q))
        share(1, q, left)
        share(2, q, right)
        v_far(q)
    for j in range(Y_FIRST, N_CHUNK):
        y_own(j)
    for q in range(N_Q):
        got("y_t", q, t_slot(across, q))
        put("xp_y", q, t_slot(across, q), t_slot(across, q))
        put("xm_y", q, t_slot(across, q), t_slot(across, q))
        share(3, q, across)
        v_far(N_Q + q)

    far = at_col(2)
    for q in range(N_Q):
        if q < N_Q // 2:
            got("xp_far", q, t_slot(far, q))
        else:
            got("xm_far", q - N_Q // 2, t_slot(far, q))
        share(4, q, far)

    pair = at_row(0, True)
    opposite = at_row(2)

    def far_on(j):
        got("zp_far", j, v_slot(j, opposite, 0, 128))
        got("zm_far", j, v_slot(j, opposite, 128, 128))
        put("y_far", j, v_slot(j, opposite), v_slot(j, opposite))

    y_left, y_right, y_far = at_col(3, True), at_col(1, True), at_col(2, True)
    for j in range(N_CHUNK):
        got("y_own", j, v_slot(j, pair))
        put("zp_pair", j, v_slot(j, pair), v_slot(j, pair))
        put("zm_pair", j, v_slot(j, pair), v_slot(j, pair))
        if j < N_Q:
            q = j
            got("xp_y", q, t_slot(y_left, q))
            got("xm_y", q, t_slot(y_right, q))
            if q < N_Q // 2:
                put("xp_yfar", q, t_slot(y_left, q), t_slot(y_left, q))
            else:
                put("xm_yfar", q - N_Q // 2, t_slot(y_right, q), t_slot(y_right, q))
            share(5, q, y_left)
            share(6, q, y_right)
        else:
            far_on(2 * (j - N_Q))
            far_on(2 * (j - N_Q) + 1)
    for q in range(N_Q):
        if q < N_Q // 2:
            got("xp_yfar", q, t_slot(y_far, q))
        else:
            got("xm_yfar", q - N_Q // 2, t_slot(y_far, q))
        share(7, q, y_far)

    other = [at_col(dx, flip, True) for dx, flip in
             ((0, False), (3, False), (1, False), (0, True), (2, False), (3, True), (1, True), (2, True))]
    for n in range(8):
        for q in range(N_Q):
            got("core", n * N_Q + q, t_slot(other[n], q))
    keep_t.wait()
    for copy in keep_v:
        copy.wait()

    def chunk_here(j):
        got("zp_pair", j, v_slot(j, at_row(3, True)))
        got("zm_pair", j, v_slot(j, at_row(1, True)))
        got("y_far", j, v_slot(j, at_row(2, True)))

    for j in range(N_CHUNK):
        chunk_here(j)
        if j < EARLY:
            early[j] = product(t_all, v_all, j, slice(None))
    for copy in started:
        copy.wait_send()


def last_kernel(t_all, v_all, early, out, tail, sems):
    copies = [
        pltpu.make_async_copy(early.at[j], out.at[:, pl.ds(j * CHUNK, CHUNK)], sems.at[j]) for j in range(EARLY)
    ]
    for copy in copies:
        copy.start()
    for j in range(EARLY, N_CHUNK):
        for m in range(2):
            rows = pl.ds(m * (IJ // 2), IJ // 2)
            tail[j - EARLY, rows, :] = product(t_all, v_all, j, rows)
            copy = pltpu.make_async_copy(
                tail.at[j - EARLY, rows, :], out.at[rows, pl.ds(j * CHUNK, CHUNK)],
                sems.at[EARLY + 2 * (j - EARLY) + m],
            )
            copy.start()
            copies.append(copy)
    for copy in copies:
        copy.wait()


def body(t2_amps, v_ints, t2_mask, v_mask):
    bf16 = jnp.bfloat16
    vmem = pl.BlockSpec(memory_space=pltpu.VMEM)
    hbm = pl.BlockSpec(memory_space=pltpu.HBM)
    smem = pl.BlockSpec(memory_space=pltpu.SMEM)
    t_own, v_own = pl.pallas_call(
        mask_kernel,
        out_shape=(pltpu.VMEM((IJ, TILE), bf16), pltpu.VMEM((N_CHUNK, PIECE, CHUNK), bf16)),
        in_specs=[smem, smem, hbm, hbm],
        out_specs=(vmem, vmem),
        scratch_shapes=[
            pltpu.VMEM((IJ, TILE), bf16),
            pltpu.VMEM((PIECE, N_CHUNK * CHUNK), bf16),
            pltpu.SemaphoreType.DMA((PIECE // TILE + N_Q,)),
        ],
        compiler_params=pltpu.CompilerParams(vmem_limit_bytes=62 * 2**20),
        name="mask",
    )(t2_mask.reshape(IJ // TILE), v_mask, t2_amps, v_ints)
    inside = lambda a: pltpu.with_memory_space_constraint(a, pltpu.VMEM)
    t_all, v_all, early = pl.pallas_call(
        gather_kernel,
        out_shape=(
            pltpu.VMEM((CD // TILE, IJ, TILE), bf16),
            pltpu.VMEM((N_CHUNK, CD, CHUNK), bf16),
            pltpu.VMEM((EARLY, IJ, CHUNK), bf16),
        ),
        in_specs=[vmem, vmem],
        out_specs=(vmem, vmem, vmem),
        scratch_shapes=[
            pltpu.VMEM((IJ, TILE), bf16),
            pltpu.SemaphoreType.DMA((N_COPIES,)),
            pltpu.SemaphoreType.DMA((N_COPIES,)),
            pltpu.SemaphoreType.DMA((1 + N_CHUNK,)),
        ],
        compiler_params=pltpu.CompilerParams(
            collective_id=0, has_side_effects=True, vmem_limit_bytes=16 * 2**20
        ),
        name="gather",
    )(inside(t_own), inside(v_own))
    return pl.pallas_call(
        last_kernel,
        out_shape=jax.ShapeDtypeStruct((IJ, N_CHUNK * CHUNK), bf16),
        in_specs=[vmem, vmem, vmem],
        out_specs=pl.BlockSpec(memory_space=pl.ANY),
        scratch_shapes=[
            pltpu.VMEM((N_CHUNK - EARLY, IJ, CHUNK), bf16),
            pltpu.SemaphoreType.DMA((EARLY + 2 * (N_CHUNK - EARLY),)),
        ],
        compiler_params=pltpu.CompilerParams(vmem_limit_bytes=16 * 2**20),
        name="last",
    )(inside(t_all), inside(v_all), inside(early))


def solution(mesh):
    in_specs = (P("row", "col"), P("row", "col"), P("row", "col"), P("row", "col"))
    out_specs = P("row", "col")
    return jax.shard_map(body, mesh=mesh, in_specs=in_specs, out_specs=out_specs, check_vma=False)
```

```python
import jax
import jax.numpy as jnp
from jax import lax
from jax.experimental import pallas as pl
from jax.experimental.pallas import tpu as pltpu
from jax.sharding import PartitionSpec as P

TILE = 128
CHUNK = 256
N_CHUNK = 8
Y_FIRST = 3
PIECE = 256
QROWS = 512
N_Q = 4
CD = 2048
IJ = 2048
MESH = pl.DeviceIdType.MESH


def mask_kernel(t2_mask, v_mask, t2_hbm, v_hbm, t2_out, v_out, t2, v, sems):
    v_in = [
        pltpu.make_async_copy(v_hbm.at[pl.ds(i * TILE, TILE), :], v.at[pl.ds(i * TILE, TILE), :], sems.at[i])
        for i in range(PIECE // TILE)
    ]
    t_in = [
        pltpu.make_async_copy(
            t2_hbm.at[pl.ds(q * QROWS, QROWS), :], t2.at[pl.ds(q * QROWS, QROWS), :], sems.at[PIECE // TILE + q]
        )
        for q in range(N_Q)
    ]
    for copy in t_in + v_in:
        copy.start()
    for i in range(IJ // TILE):
        if i % (QROWS // TILE) == 0:
            t_in[i // (QROWS // TILE)].wait()
        rows = pl.ds(i * TILE, TILE)
        block = t2[rows, :]
        t2_out[rows, :] = jnp.where(t2_mask[i] > 0, block, jnp.zeros_like(block))
    for i in range(PIECE // TILE):
        v_in[i].wait()
        rows = pl.ds(i * TILE, TILE)
        for j in range(N_CHUNK):
            for b in range(CHUNK // TILE):
                block = v[rows, pl.ds(j * CHUNK + b * TILE, TILE)]
                kept = v_mask[i, j * (CHUNK // TILE) + b] > 0
                v_out[j, rows, pl.ds(b * TILE, TILE)] = jnp.where(kept, block, jnp.zeros_like(block))


def product(t_all, v_all, j, rows, pieces):
    amps = jnp.concatenate([t_all[2 * p + h, rows, :] for p in pieces for h in range(2)], axis=1)
    ints = jnp.concatenate(
        [v_all[j, pl.ds(pl.multiple_of(p * PIECE, PIECE), PIECE), :] for p in pieces], axis=0
    )
    return jnp.dot(amps, ints, preferred_element_type=jnp.float32)


COPIES = {
    "zp_own": N_CHUNK, "zm_own": N_CHUNK, "zp_far": N_CHUNK, "zm_far": N_CHUNK,
    "zp_pair": N_CHUNK, "zm_pair": N_CHUNK, "y_own": N_CHUNK, "y_far": N_CHUNK,
    "b_t": N_Q, "y_t": N_Q, "xp_own": N_Q, "xm_own": N_Q, "xp_y": N_Q, "xm_y": N_Q,
    "xp_far": N_Q // 2, "xm_far": N_Q // 2, "xp_yfar": N_Q // 2, "xm_yfar": N_Q // 2,
    "core": 8 * N_Q,
}
FIRST = {}
for _name, _count in COPIES.items():
    FIRST[_name] = sum(COPIES[n] for n in list(COPIES)[: list(COPIES).index(_name)])
N_COPIES = sum(COPIES.values())


def gather_kernel(t_own, v_own, early, t_all, v_all, partial, relay, send, recv, local):
    row, col = lax.axis_index("row"), lax.axis_index("col")
    z, y_lo = row // 2, row % 2
    x, y_hi, core = col // 4, (col // 2) % 2, col % 2

    def at_row(dz, flip=False):
        return ((z + dz) % 4) * 2 + (1 - y_lo if flip else y_lo)

    def at_col(dx, flip=False, other=False):
        return ((x + dx) % 4) * 4 + (1 - y_hi if flip else y_hi) * 2 + (1 - core if other else core)

    to = {
        "zp": (at_row(1), col), "zm": (at_row(3), col), "y": (at_row(0, True), col),
        "xp": (row, at_col(1)), "xm": (row, at_col(3)), "b": (at_row(0, True), at_col(0, True)),
        "core": (row, at_col(0, False, True)),
    }

    def v_slot(j, piece, first=0, count=PIECE):
        return v_all.at[j, pl.ds(pl.multiple_of(piece * PIECE + first, 128), count), :]

    def t_slot(piece, q):
        return t_all.at[piece, pl.ds(q * QROWS, QROWS), :]

    started = []

    def describe(name, n, src, dst):
        i = FIRST[name] + n
        return pltpu.make_async_remote_copy(
            src_ref=src, dst_ref=dst, send_sem=send.at[i], recv_sem=recv.at[i],
            device_id=to[name.split("_")[0]], device_id_type=MESH,
        )

    def put(name, n, src, dst):
        copy = describe(name, n, src, dst)
        copy.start()
        started.append(copy)

    def got(name, n, slot):
        describe(name, n, slot, slot).wait_recv()

    def share(n, q, piece, src=None):
        put("core", n * N_Q + q, t_slot(piece, q) if src is None else src, t_slot(piece, q))

    keep_t = pltpu.make_async_copy(t_own, t_all.at[col], local.at[0])
    keep_v = [pltpu.make_async_copy(v_own.at[j], v_slot(j, row), local.at[1 + j]) for j in range(N_CHUNK)]

    barrier = pltpu.get_barrier_semaphore()
    for device in to.values():
        pl.semaphore_signal(barrier, inc=1, device_id=device, device_id_type=MESH)
    keep_t.start()
    for copy in keep_v:
        copy.start()
    pl.semaphore_wait(barrier, len(to))

    def own_q(q):
        return t_own.at[pl.ds(q * QROWS, QROWS), :]

    def relay_q(q):
        return relay.at[pl.ds(q * QROWS, QROWS), :]

    def y_own(j):
        put("y_own", j, v_own.at[j], v_slot(j, row))

    for j in range(Y_FIRST):
        y_own(j)
    for q in range(N_Q):
        put("b_t", q, own_q(q), relay_q(q))
    for j in range(N_CHUNK):
        put("zp_own", j, v_own.at[j], v_slot(j, row))
        put("zm_own", j, v_own.at[j], v_slot(j, row))
    for q in range(N_Q):
        put("xp_own", q, own_q(q), t_slot(col, q))
        put("xm_own", q, own_q(q), t_slot(col, q))
    for q in range(N_Q):
        share(0, q, col, own_q(q))

    below, above = at_row(3), at_row(1)
    left, right = at_col(3), at_col(1)
    across = at_col(0, True)

    def v_far(j):
        got("zp_own", j, v_slot(j, below))
        got("zm_own", j, v_slot(j, above))
        put("zp_far", j, v_slot(j, below, 0, 128), v_slot(j, below, 0, 128))
        put("zm_far", j, v_slot(j, above, 128, 128), v_slot(j, above, 128, 128))

    for q in range(N_Q):
        got("b_t", q, relay_q(q))
        put("y_t", q, relay_q(q), t_slot(across, q))
        got("xp_own", q, t_slot(left, q))
        got("xm_own", q, t_slot(right, q))
        if q < N_Q // 2:
            put("xp_far", q, t_slot(left, q), t_slot(left, q))
        else:
            put("xm_far", q - N_Q // 2, t_slot(right, q), t_slot(right, q))
        share(1, q, left)
        share(2, q, right)
        v_far(q)
    for j in range(Y_FIRST, N_CHUNK):
        y_own(j)
    for q in range(N_Q):
        got("y_t", q, t_slot(across, q))
        put("xp_y", q, t_slot(across, q), t_slot(across, q))
        put("xm_y", q, t_slot(across, q), t_slot(across, q))
        share(3, q, across)
        v_far(N_Q + q)

    far = at_col(2)
    for q in range(N_Q):
        if q < N_Q // 2:
            got("xp_far", q, t_slot(far, q))
        else:
            got("xm_far", q - N_Q // 2, t_slot(far, q))
        share(4, q, far)

    pair = at_row(0, True)
    opposite = at_row(2)

    def far_on(j):
        got("zp_far", j, v_slot(j, opposite, 0, 128))
        got("zm_far", j, v_slot(j, opposite, 128, 128))
        put("y_far", j, v_slot(j, opposite), v_slot(j, opposite))

    y_left, y_right, y_far = at_col(3, True), at_col(1, True), at_col(2, True)
    for j in range(N_CHUNK):
        got("y_own", j, v_slot(j, pair))
        put("zp_pair", j, v_slot(j, pair), v_slot(j, pair))
        put("zm_pair", j, v_slot(j, pair), v_slot(j, pair))
        if j < N_Q:
            q = j
            got("xp_y", q, t_slot(y_left, q))
            got("xm_y", q, t_slot(y_right, q))
            if q < N_Q // 2:
                put("xp_yfar", q, t_slot(y_left, q), t_slot(y_left, q))
            else:
                put("xm_yfar", q - N_Q // 2, t_slot(y_right, q), t_slot(y_right, q))
            share(5, q, y_left)
            share(6, q, y_right)
        else:
            far_on(2 * (j - N_Q))
            far_on(2 * (j - N_Q) + 1)
    for q in range(N_Q):
        if q < N_Q // 2:
            got("xp_yfar", q, t_slot(y_far, q))
        else:
            got("xm_yfar", q - N_Q // 2, t_slot(y_far, q))
        share(7, q, y_far)

    other = [at_col(dx, flip, True) for dx, flip in
             ((0, False), (3, False), (1, False), (0, True), (2, False), (3, True), (1, True), (2, True))]
    for n in range(8):
        for q in range(N_Q):
            got("core", n * N_Q + q, t_slot(other[n], q))
    keep_t.wait()
    for copy in keep_v:
        copy.wait()

    def chunk_here(j):
        got("zp_pair", j, v_slot(j, at_row(3, True)))
        got("zm_pair", j, v_slot(j, at_row(1, True)))
        got("y_far", j, v_slot(j, at_row(2, True)))

    for j in range(N_CHUNK):
        for q in range(N_Q):
            rows = pl.ds(q * QROWS, QROWS)
            partial[j, rows, :] = product(t_all, v_all, j, rows, (row, below, above, opposite, pair))
    late = (at_row(3, True), at_row(1, True), at_row(2, True))
    for j in range(N_CHUNK):
        chunk_here(j)
        for q in range(N_Q):
            rows = pl.ds(q * QROWS, QROWS)
            whole = partial[j, rows, :] + product(t_all, v_all, j, rows, late)
            early[j, rows, :] = whole.astype(jnp.bfloat16)
    for copy in started:
        copy.wait_send()


def last_kernel(early, out, sems):
    copies = [
        pltpu.make_async_copy(early.at[j], out.at[:, pl.ds(j * CHUNK, CHUNK)], sems.at[j]) for j in range(N_CHUNK)
    ]
    for copy in copies:
        copy.start()
    for copy in copies:
        copy.wait()


def body(t2_amps, v_ints, t2_mask, v_mask):
    bf16 = jnp.bfloat16
    vmem = pl.BlockSpec(memory_space=pltpu.VMEM)
    hbm = pl.BlockSpec(memory_space=pltpu.HBM)
    smem = pl.BlockSpec(memory_space=pltpu.SMEM)
    t_own, v_own = pl.pallas_call(
        mask_kernel,
        out_shape=(pltpu.VMEM((IJ, TILE), bf16), pltpu.VMEM((N_CHUNK, PIECE, CHUNK), bf16)),
        in_specs=[smem, smem, hbm, hbm],
        out_specs=(vmem, vmem),
        scratch_shapes=[
            pltpu.VMEM((IJ, TILE), bf16),
            pltpu.VMEM((PIECE, N_CHUNK * CHUNK), bf16),
            pltpu.SemaphoreType.DMA((PIECE // TILE + N_Q,)),
        ],
        compiler_params=pltpu.CompilerParams(vmem_limit_bytes=62 * 2**20),
        name="mask",
    )(t2_mask.reshape(IJ // TILE), v_mask, t2_amps, v_ints)
    inside = lambda a: pltpu.with_memory_space_constraint(a, pltpu.VMEM)
    early = pl.pallas_call(
        gather_kernel,
        out_shape=pltpu.VMEM((N_CHUNK, IJ, CHUNK), bf16),
        in_specs=[vmem, vmem],
        out_specs=vmem,
        scratch_shapes=[
            pltpu.VMEM((CD // TILE, IJ, TILE), bf16),
            pltpu.VMEM((N_CHUNK, CD, CHUNK), bf16),
            pltpu.VMEM((N_CHUNK, IJ, CHUNK), jnp.float32),
            pltpu.VMEM((IJ, TILE), bf16),
            pltpu.SemaphoreType.DMA((N_COPIES,)),
            pltpu.SemaphoreType.DMA((N_COPIES,)),
            pltpu.SemaphoreType.DMA((1 + N_CHUNK,)),
        ],
        compiler_params=pltpu.CompilerParams(
            collective_id=0, has_side_effects=True, vmem_limit_bytes=48 * 2**20
        ),
        name="gather",
    )(inside(t_own), inside(v_own))
    return pl.pallas_call(
        last_kernel,
        out_shape=jax.ShapeDtypeStruct((IJ, N_CHUNK * CHUNK), bf16),
        in_specs=[vmem],
        out_specs=pl.BlockSpec(memory_space=pl.ANY),
        scratch_shapes=[pltpu.SemaphoreType.DMA((N_CHUNK,))],
        compiler_params=pltpu.CompilerParams(vmem_limit_bytes=16 * 2**20),
        name="last",
    )(inside(early))


def solution(mesh):
    in_specs = (P("row", "col"), P("row", "col"), P("row", "col"), P("row", "col"))
    out_specs = P("row", "col")
    return jax.shard_map(body, mesh=mesh, in_specs=in_specs, out_specs=out_specs, check_vma=False)
```

```python
import jax
import jax.numpy as jnp
from jax import lax
from jax.experimental import pallas as pl
from jax.experimental.pallas import tpu as pltpu
from jax.sharding import PartitionSpec as P

TILE = 128
CHUNK = 256
N_CHUNK = 8
Y_FIRST = 3
PIECE = 256
QROWS = 512
N_Q = 4
CD = 2048
IJ = 2048
MESH = pl.DeviceIdType.MESH


def mask_kernel(t2_mask, v_mask, t2_hbm, v_hbm, t2_out, v_out, t2, v, sems):
    v_in = [
        pltpu.make_async_copy(v_hbm.at[pl.ds(i * TILE, TILE), :], v.at[pl.ds(i * TILE, TILE), :], sems.at[i])
        for i in range(PIECE // TILE)
    ]
    t_in = [
        pltpu.make_async_copy(
            t2_hbm.at[pl.ds(q * QROWS, QROWS), :], t2.at[pl.ds(q * QROWS, QROWS), :], sems.at[PIECE // TILE + q]
        )
        for q in range(N_Q)
    ]
    for copy in t_in + v_in:
        copy.start()
    for i in range(IJ // TILE):
        if i % (QROWS // TILE) == 0:
            t_in[i // (QROWS // TILE)].wait()
        rows = pl.ds(i * TILE, TILE)
        block = t2[rows, :]
        t2_out[rows, :] = jnp.where(t2_mask[i] > 0, block, jnp.zeros_like(block))
    for i in range(PIECE // TILE):
        v_in[i].wait()
        rows = pl.ds(i * TILE, TILE)
        for j in range(N_CHUNK):
            for b in range(CHUNK // TILE):
                block = v[rows, pl.ds(j * CHUNK + b * TILE, TILE)]
                kept = v_mask[i, j * (CHUNK // TILE) + b] > 0
                v_out[j, rows, pl.ds(b * TILE, TILE)] = jnp.where(kept, block, jnp.zeros_like(block))


def product(t_all, v_all, j, rows, pieces):
    amps = jnp.concatenate([t_all[2 * p + h, rows, :] for p in pieces for h in range(2)], axis=1)
    ints = jnp.concatenate(
        [v_all[j, pl.ds(pl.multiple_of(p * PIECE, PIECE), PIECE), :] for p in pieces], axis=0
    )
    return jnp.dot(amps, ints, preferred_element_type=jnp.float32)


COPIES = {
    "zp_own": N_CHUNK, "zm_own": N_CHUNK, "zp_far": N_CHUNK, "zm_far": N_CHUNK,
    "zp_pair": N_CHUNK, "zm_pair": N_CHUNK, "y_own": N_CHUNK, "y_far": N_CHUNK,
    "b_t": N_Q, "y_t": N_Q, "xp_own": N_Q, "xm_own": N_Q, "xp_y": N_Q, "xm_y": N_Q,
    "xp_far": N_Q // 2, "xm_far": N_Q // 2, "xp_yfar": N_Q // 2, "xm_yfar": N_Q // 2,
    "core": 8 * N_Q,
}
FIRST = {}
for _name, _count in COPIES.items():
    FIRST[_name] = sum(COPIES[n] for n in list(COPIES)[: list(COPIES).index(_name)])
N_COPIES = sum(COPIES.values())


def gather_kernel(t_own, v_own, early, t_all, v_all, partial, relay, send, recv, local):
    row, col = lax.axis_index("row"), lax.axis_index("col")
    z, y_lo = row // 2, row % 2
    x, y_hi, core = col // 4, (col // 2) % 2, col % 2

    def at_row(dz, flip=False):
        return ((z + dz) % 4) * 2 + (1 - y_lo if flip else y_lo)

    def at_col(dx, flip=False, other=False):
        return ((x + dx) % 4) * 4 + (1 - y_hi if flip else y_hi) * 2 + (1 - core if other else core)

    to = {
        "zp": (at_row(1), col), "zm": (at_row(3), col), "y": (at_row(0, True), col),
        "xp": (row, at_col(1)), "xm": (row, at_col(3)), "b": (at_row(0, True), at_col(0, True)),
        "core": (row, at_col(0, False, True)),
    }

    def v_slot(j, piece, first=0, count=PIECE):
        return v_all.at[j, pl.ds(pl.multiple_of(piece * PIECE + first, 128), count), :]

    def t_slot(piece, q):
        return t_all.at[piece, pl.ds(q * QROWS, QROWS), :]

    started = []

    def describe(name, n, src, dst):
        i = FIRST[name] + n
        return pltpu.make_async_remote_copy(
            src_ref=src, dst_ref=dst, send_sem=send.at[i], recv_sem=recv.at[i],
            device_id=to[name.split("_")[0]], device_id_type=MESH,
        )

    def put(name, n, src, dst):
        copy = describe(name, n, src, dst)
        copy.start()
        started.append(copy)

    def got(name, n, slot):
        describe(name, n, slot, slot).wait_recv()

    def share(n, q, piece, src=None):
        put("core", n * N_Q + q, t_slot(piece, q) if src is None else src, t_slot(piece, q))

    keep_t = pltpu.make_async_copy(t_own, t_all.at[col], local.at[0])
    keep_v = [pltpu.make_async_copy(v_own.at[j], v_slot(j, row), local.at[1 + j]) for j in range(N_CHUNK)]

    barrier = pltpu.get_barrier_semaphore()
    for device in to.values():
        pl.semaphore_signal(barrier, inc=1, device_id=device, device_id_type=MESH)
    keep_t.start()
    for copy in keep_v:
        copy.start()
    pl.semaphore_wait(barrier, len(to))

    def own_q(q):
        return t_own.at[pl.ds(q * QROWS, QROWS), :]

    def relay_q(q):
        return relay.at[pl.ds(q * QROWS, QROWS), :]

    def y_own(j):
        put("y_own", j, v_own.at[j], v_slot(j, row))

    for j in range(Y_FIRST):
        y_own(j)
    for q in range(N_Q):
        put("b_t", q, own_q(q), relay_q(q))
    for j in range(N_CHUNK):
        put("zp_own", j, v_own.at[j], v_slot(j, row))
        put("zm_own", j, v_own.at[j], v_slot(j, row))
    for q in range(N_Q):
        put("xp_own", q, own_q(q), t_slot(col, q))
        put("xm_own", q, own_q(q), t_slot(col, q))
    for q in range(N_Q):
        share(0, q, col, own_q(q))

    below, above = at_row(3), at_row(1)
    left, right = at_col(3), at_col(1)
    across = at_col(0, True)

    def v_far(j):
        got("zp_own", j, v_slot(j, below))
        got("zm_own", j, v_slot(j, above))
        put("zp_far", j, v_slot(j, below, 0, 128), v_slot(j, below, 0, 128))
        put("zm_far", j, v_slot(j, above, 128, 128), v_slot(j, above, 128, 128))

    for q in range(N_Q):
        got("b_t", q, relay_q(q))
        put("y_t", q, relay_q(q), t_slot(across, q))
        got("xp_own", q, t_slot(left, q))
        got("xm_own", q, t_slot(right, q))
        if q < N_Q // 2:
            put("xp_far", q, t_slot(left, q), t_slot(left, q))
        else:
            put("xm_far", q - N_Q // 2, t_slot(right, q), t_slot(right, q))
        share(1, q, left)
        share(2, q, right)
        v_far(q)
    for j in range(Y_FIRST, N_CHUNK):
        y_own(j)
    for q in range(N_Q):
        got("y_t", q, t_slot(across, q))
        put("xp_y", q, t_slot(across, q), t_slot(across, q))
        put("xm_y", q, t_slot(across, q), t_slot(across, q))
        share(3, q, across)
        v_far(N_Q + q)

    far = at_col(2)
    for q in range(N_Q):
        if q < N_Q // 2:
            got("xp_far", q, t_slot(far, q))
        else:
            got("xm_far", q - N_Q // 2, t_slot(far, q))
        share(4, q, far)

    pair = at_row(0, True)
    opposite = at_row(2)

    def far_on(j):
        got("zp_far", j, v_slot(j, opposite, 0, 128))
        got("zm_far", j, v_slot(j, opposite, 128, 128))
        put("y_far", j, v_slot(j, opposite), v_slot(j, opposite))

    y_left, y_right, y_far = at_col(3, True), at_col(1, True), at_col(2, True)
    for j in range(N_CHUNK):
        if j < N_Q:
            q = j
            got("xp_y", q, t_slot(y_left, q))
            got("xm_y", q, t_slot(y_right, q))
            if q < N_Q // 2:
                put("xp_yfar", q, t_slot(y_left, q), t_slot(y_left, q))
            else:
                put("xm_yfar", q - N_Q // 2, t_slot(y_right, q), t_slot(y_right, q))
            share(5, q, y_left)
            share(6, q, y_right)
        far_on(j)
        got("y_own", j, v_slot(j, pair))
        put("zp_pair", j, v_slot(j, pair), v_slot(j, pair))
        put("zm_pair", j, v_slot(j, pair), v_slot(j, pair))
    for q in range(N_Q):
        if q < N_Q // 2:
            got("xp_yfar", q, t_slot(y_far, q))
        else:
            got("xm_yfar", q - N_Q // 2, t_slot(y_far, q))
        share(7, q, y_far)

    other = [at_col(dx, flip, True) for dx, flip in
             ((0, False), (3, False), (1, False), (0, True), (2, False), (3, True), (1, True), (2, True))]
    for n in range(8):
        for q in range(N_Q):
            got("core", n * N_Q + q, t_slot(other[n], q))
    keep_t.wait()
    for copy in keep_v:
        copy.wait()

    def chunk_here(j):
        got("zp_pair", j, v_slot(j, at_row(3, True)))
        got("zm_pair", j, v_slot(j, at_row(1, True)))
        got("y_far", j, v_slot(j, at_row(2, True)))

    for j in range(N_CHUNK):
        for q in range(N_Q):
            rows = pl.ds(q * QROWS, QROWS)
            partial[j, rows, :] = product(t_all, v_all, j, rows, (row, below, above, opposite, pair))
    late = (at_row(3, True), at_row(1, True), at_row(2, True))
    for j in range(N_CHUNK):
        chunk_here(j)
        for q in range(N_Q):
            rows = pl.ds(q * QROWS, QROWS)
            whole = partial[j, rows, :] + product(t_all, v_all, j, rows, late)
            early[rows, pl.ds(j * CHUNK, CHUNK)] = whole.astype(jnp.bfloat16)
    for copy in started:
        copy.wait_send()


def last_kernel(early, out, sems):
    copies = [
        pltpu.make_async_copy(early.at[pl.ds(j * 256, 256), :], out.at[pl.ds(j * 256, 256), :], sems.at[j])
        for j in range(N_CHUNK)
    ]
    for copy in copies:
        copy.start()
    for copy in copies:
        copy.wait()


def body(t2_amps, v_ints, t2_mask, v_mask):
    bf16 = jnp.bfloat16
    vmem = pl.BlockSpec(memory_space=pltpu.VMEM)
    hbm = pl.BlockSpec(memory_space=pltpu.HBM)
    smem = pl.BlockSpec(memory_space=pltpu.SMEM)
    t_own, v_own = pl.pallas_call(
        mask_kernel,
        out_shape=(pltpu.VMEM((IJ, TILE), bf16), pltpu.VMEM((N_CHUNK, PIECE, CHUNK), bf16)),
        in_specs=[smem, smem, hbm, hbm],
        out_specs=(vmem, vmem),
        scratch_shapes=[
            pltpu.VMEM((IJ, TILE), bf16),
            pltpu.VMEM((PIECE, N_CHUNK * CHUNK), bf16),
            pltpu.SemaphoreType.DMA((PIECE // TILE + N_Q,)),
        ],
        compiler_params=pltpu.CompilerParams(vmem_limit_bytes=62 * 2**20),
        name="mask",
    )(t2_mask.reshape(IJ // TILE), v_mask, t2_amps, v_ints)
    inside = lambda a: pltpu.with_memory_space_constraint(a, pltpu.VMEM)
    early = pl.pallas_call(
        gather_kernel,
        out_shape=pltpu.VMEM((IJ, N_CHUNK * CHUNK), bf16),
        in_specs=[vmem, vmem],
        out_specs=vmem,
        scratch_shapes=[
            pltpu.VMEM((CD // TILE, IJ, TILE), bf16),
            pltpu.VMEM((N_CHUNK, CD, CHUNK), bf16),
            pltpu.VMEM((N_CHUNK, IJ, CHUNK), jnp.float32),
            pltpu.VMEM((IJ, TILE), bf16),
            pltpu.SemaphoreType.DMA((N_COPIES,)),
            pltpu.SemaphoreType.DMA((N_COPIES,)),
            pltpu.SemaphoreType.DMA((1 + N_CHUNK,)),
        ],
        compiler_params=pltpu.CompilerParams(
            collective_id=0, has_side_effects=True, vmem_limit_bytes=48 * 2**20
        ),
        name="gather",
    )(inside(t_own), inside(v_own))
    return pl.pallas_call(
        last_kernel,
        out_shape=jax.ShapeDtypeStruct((IJ, N_CHUNK * CHUNK), bf16),
        in_specs=[vmem],
        out_specs=pl.BlockSpec(memory_space=pl.ANY),
        scratch_shapes=[pltpu.SemaphoreType.DMA((N_CHUNK,))],
        compiler_params=pltpu.CompilerParams(vmem_limit_bytes=16 * 2**20),
        name="last",
    )(inside(early))


def solution(mesh):
    in_specs = (P("row", "col"), P("row", "col"), P("row", "col"), P("row", "col"))
    out_specs = P("row", "col")
    return jax.shard_map(body, mesh=mesh, in_specs=in_specs, out_specs=out_specs, check_vma=False)
```
